32 devices in a mesh: grp: 4 (over z), cp: 8 (over y, x, core).
Axes of the slice: x: 2, y: 2, z: 4, core: 2. Of those that a mesh axis runs over, the one named last changes fastest.
Arguments:
- query_proj: bfloat16 [4096, 4096], P(('grp', 'cp')), may hold values from -6 to 6
- key_proj: bfloat16 [4096, 512], P(('grp', 'cp')), may hold values from -6 to 6
- value_projection: bfloat16 [4096, 512], P(('grp', 'cp')), may hold values from -6 to 6
- segment_ids: int32 [4096], P(('grp', 'cp')), may hold values from 0 to 15, never falling along the last dimension, each value on 1 to 1024 neighbouring positions
Outputs:
- attended: bfloat16 [4096, 4096], P(('grp', 'cp'))
The draws below stay inside these ranges and needn't reach their ends.
Inputs may be any that keep to these rules, and one draw needn't show every extreme that they name: `segment_ids`: never falls along the stream; every document has 1 to 1024 tokens, and one has exactly 1024.
All inputs are finite; a program needn't handle non-finite values.
Results may differ from the reference program's by a relative error of at most 0.0034.
Values may be sent and summed in bfloat16 or wider, within the bound.
A program may use at most 64 MiB of HBM per device.

```python
import math
import jax
import jax.numpy as jnp
import numpy as np
from jax import lax

QUERY_HEADS = 32
KEY_VALUE_HEADS = 4
HEAD_WIDTH = 128
TOK_DEV = 128
SPAN = 8
MOST = 1024
STREAM_TOKENS = 4096
DOCS = 16


def draw_query_proj(key, part):
    unmasked_result = jnp.clip(jax.random.normal(jax.random.fold_in(key, 11), (STREAM_TOKENS, QUERY_HEADS * HEAD_WIDTH), jnp.float32), -6.0, 6.0)
    return unmasked_result.astype(jnp.bfloat16)


def draw_key_proj(key, part):
    unmasked_result = jnp.clip(jax.random.normal(jax.random.fold_in(key, 12), (STREAM_TOKENS, KEY_VALUE_HEADS * HEAD_WIDTH), jnp.float32), -6.0, 6.0)
    return unmasked_result.astype(jnp.bfloat16)


def levels(rng, dims, split, smallest, high):
    loudness = 1.0
    for dim, blocks in split:
        steps = jax.random.uniform(jax.random.fold_in(jax.random.fold_in(rng, 6), dim), (blocks,), jnp.float32, smallest / len(split), high / len(split))
        loudness = loudness * jnp.repeat(jnp.exp(steps), dims[dim] // blocks).reshape((-1,) + (1,) * (len(dims) - 1 - dim))
    return loudness


def profile(count, total, bound, skew):
    portions = [(1 << 20) // math.isqrt(rank ** skew) + 1 for rank in range(2, count + 1)]
    spare, counts = total - bound - (count - 1), [1] * (count - 1)
    while spare > 0:
        candidates = [i for i in range(count - 1) if counts[i] < bound]
        whole, budget = sum([portions[i] for i in candidates]), spare
        for i in candidates:
            addition = min(bound - counts[i], max(1, budget * portions[i] // whole), spare)
            counts[i] = counts[i] + addition
            spare = spare - addition
    return np.array([bound] + counts)


def ragged(own_key, amount, total, reach, lean):
    if amount == 2:
        one = jax.random.randint(own_key, (), max(1, total - reach), min(reach, total - 1) + 1)
        return jnp.stack([one, total - one])
    lengths = jnp.asarray(profile(amount, total, reach, lean), jnp.int32)
    twos = (amount - 1) // 2
    giver, taker = lengths[1:1 + 2 * twos:2], lengths[2:2 + 2 * twos:2]
    slack = jnp.minimum(giver - 1, reach - taker)
    moved = jax.random.randint(jax.random.fold_in(own_key, 1), (twos,), 0, 1 << 20) % (slack + 1)
    lengths = lengths.at[1:1 + 2 * twos:2].set(giver - moved).at[2:2 + 2 * twos:2].set(taker + moved)
    return lengths[jax.random.permutation(jax.random.fold_in(own_key, 2), amount)]


def scatter_about(stream_key, dims, spread, reach, pieces=(), kind=jnp.bfloat16):
    gain = levels(stream_key, dims, pieces, -0.22, 0.18) if pieces else 1.0
    result = jax.random.normal(stream_key, dims, jnp.float32) * spread * gain
    return jnp.minimum(jnp.maximum(result, -reach), reach).astype(kind)


def setup_inputs(seed: int = 0) -> dict:
    key_list = jax.random.split(jax.random.key(seed), 5)
    return {
        "query_proj": draw_query_proj(jax.random.fold_in(key_list[4], 71), 0),
        "key_proj": draw_key_proj(jax.random.fold_in(key_list[4], 71), 0),
        "value_projection": scatter_about(key_list[2], (STREAM_TOKENS, KEY_VALUE_HEADS * HEAD_WIDTH), 1.0, 6.0, ((0, 32),)),
        "segment_ids": jnp.searchsorted(jnp.cumsum(ragged(key_list[3], DOCS, STREAM_TOKENS, MOST, 2)), jnp.arange(STREAM_TOKENS), side="right").astype(jnp.int32),
    }


def attend_window(query_rows, key_win, value_win, seg_query, seg_keys, pos_query, pos_keys):
    tok_rows = query_rows.shape[0]
    group_size = query_rows.shape[1] // key_win.shape[1]
    kv_count = key_win.shape[1] // HEAD_WIDTH
    score_scale = 1.0 / math.sqrt(HEAD_WIDTH)
    visible = (seg_query[:, None] == seg_keys[None, :]) & (pos_keys[None, :] <= pos_query[:, None]) & (pos_keys[None, :] >= 0)
    pieces_out = []
    for kv_head in range(kv_count):
        q_block = query_rows[:, kv_head * group_size * HEAD_WIDTH:(kv_head + 1) * group_size * HEAD_WIDTH].reshape(tok_rows, group_size, HEAD_WIDTH).astype(jnp.float32)
        k_block = key_win[:, kv_head * HEAD_WIDTH:(kv_head + 1) * HEAD_WIDTH].astype(jnp.float32)
        v_block = value_win[:, kv_head * HEAD_WIDTH:(kv_head + 1) * HEAD_WIDTH].astype(jnp.float32)
        scores = jnp.einsum('tgd,sd->tgs', q_block, k_block, precision=lax.Precision.HIGHEST) * score_scale
        scores = jnp.where(visible[:, None, :], scores, -jnp.inf)
        row_max = lax.optimization_barrier(jnp.max(scores, axis=2, keepdims=True))
        weights = jnp.exp(scores - row_max)
        row_total = lax.optimization_barrier(jnp.sum(weights, axis=2, keepdims=True))
        probs = lax.optimization_barrier(weights.astype(jnp.bfloat16)).astype(jnp.float32)
        mixed = jnp.einsum('tgs,sd->tgd', probs, v_block, precision=lax.Precision.HIGHEST) / row_total
        pieces_out.append(mixed.reshape(tok_rows, group_size * HEAD_WIDTH).astype(jnp.bfloat16))
    return jnp.concatenate(pieces_out, axis=1)

def reference(query_proj, key_proj, value_projection, segment_ids):
    margin = SPAN * TOK_DEV
    padded_keys = jnp.concatenate([jnp.zeros((margin, key_proj.shape[1]), key_proj.dtype), key_proj], 0)
    padded_values = jnp.concatenate([jnp.zeros((margin, value_projection.shape[1]), value_projection.dtype), value_projection], 0)
    padded_segs = jnp.concatenate([jnp.full((margin,), -1, jnp.int32), segment_ids.astype(jnp.int32)], 0)
    block_count = STREAM_TOKENS // TOK_DEV

    def one_block(block_index):
        first_pos = (block_index * TOK_DEV).astype(jnp.int32)
        query_rows = lax.dynamic_slice_in_dim(query_proj, first_pos, TOK_DEV, 0)
        seg_query = lax.dynamic_slice_in_dim(segment_ids.astype(jnp.int32), first_pos, TOK_DEV, 0)
        key_win = lax.dynamic_slice_in_dim(padded_keys, first_pos, margin + TOK_DEV, 0)
        value_win = lax.dynamic_slice_in_dim(padded_values, first_pos, margin + TOK_DEV, 0)
        seg_keys = lax.dynamic_slice_in_dim(padded_segs, first_pos, margin + TOK_DEV, 0)
        pos_query = first_pos + jnp.arange(TOK_DEV, dtype=jnp.int32)
        pos_keys = first_pos - margin + jnp.arange(margin + TOK_DEV, dtype=jnp.int32)
        return attend_window(query_rows, key_win, value_win, seg_query, seg_keys, pos_query, pos_keys)
    blocks_out = lax.map(one_block, jnp.arange(block_count, dtype=jnp.int32))
    return blocks_out.reshape(STREAM_TOKENS, QUERY_HEADS * HEAD_WIDTH)
```

```python
import functools
import math

import jax
import jax.numpy as jnp
from jax import lax
from jax.experimental import pallas as pl
from jax.experimental.pallas import tpu as pltpu
from jax.sharding import PartitionSpec as P

HEAD_WIDTH = 128
SPAN = 8
BIG = 1e30
MESH = pl.DeviceIdType.MESH
PER_STEP = 2


def kernel(
    count, cp_count, heads, group,
    q_hbm, k_hbm, v_hbm, s_hbm, o_hbm,
    kv, seg, q_buf, tri_bias, row_neg, col_bias,
    send_sem, recv_sem, in_sem, q_sem, o_sem,
):
    tok = kv.shape[3]
    flat = lax.axis_index("grp") * cp_count + lax.axis_index("cp")
    spot = lax.rem(flat, SPAN)
    base = flat - spot
    chip, core = spot // 2, lax.rem(spot, 2)
    partner = base + chip * 2 + (1 - core)
    has_prev = flat >= SPAN
    has_next = flat + SPAN < count
    chips = SPAN // 2
    others = [jnp.bitwise_xor(chip, m) for m in range(1, chips)]

    def dev(f):
        return (f // cp_count, lax.rem(f, cp_count))

    def slot_at(owner, place):
        return lax.rem(owner - place + SPAN, SPAN)

    def view(part, slot):
        return seg.at[slot] if part == 0 else kv.at[slot, part - 1]

    def remote(part, src, dst, k, target):
        return pltpu.make_async_remote_copy(
            src_ref=view(part, src), dst_ref=view(part, dst),
            send_sem=send_sem.at[part, k], recv_sem=recv_sem.at[part, dst],
            device_id=dev(target), device_id_type=MESH,
        )

    def to_next(part):
        return remote(part, SPAN, 0, 0, flat + SPAN)

    def to_chip(part, m, src):
        place = others[m] * 2 + core
        return remote(part, src, slot_at(spot, place), 1 + m, base + place)

    def to_partner(part, src):
        return remote(part, src, slot_at(spot, chip * 2 + 1 - core), chips, partner)

    def forward(part, m):
        owner = others[m] * 2 + core
        return remote(part, slot_at(owner, spot), slot_at(owner, chip * 2 + 1 - core),
                      chips + 1 + m, partner)

    def wait_slot(part, slot):
        remote(part, SPAN, slot, 0, partner).wait_recv()

    def load_in(h, which):
        ref = (k_hbm, v_hbm)[which]
        return pltpu.make_async_copy(
            ref.at[:, h * HEAD_WIDTH:(h + 1) * HEAD_WIDTH], kv.at[SPAN, h, which],
            in_sem.at[2 * h + which])

    seg_in = pltpu.make_async_copy(s_hbm, seg.at[SPAN], in_sem.at[2 * heads])
    seg_in.start()
    for h in range(heads):
        for which in range(2):
            load_in(h, which).start()
    width = group * HEAD_WIDTH

    def load_q(h):
        return pltpu.make_async_copy(
            q_hbm.at[:, h * width:(h + 1) * width], q_buf.at[:, h * width:(h + 1) * width],
            q_sem.at[h])

    for h in range(heads):
        load_q(h).start()

    barrier = pltpu.get_barrier_semaphore()

    def hello(target):
        pl.semaphore_signal(barrier, inc=1, device_id=dev(target), device_id_type=MESH)

    hello(partner)
    for o in others:
        hello(base + o * 2 + core)

    @pl.when(has_prev)
    def _():
        hello(flat - SPAN)

    @pl.when(has_next)
    def _():
        hello(flat + SPAN)

    @pl.when(jnp.logical_not(has_prev))
    def _():
        for r in range(SPAN):
            @pl.when(spot + r < SPAN)
            def _():
                kv[r] = jnp.zeros(kv.shape[1:], kv.dtype)
                seg[r] = jnp.full(seg.shape[1:], -1, seg.dtype)

    pl.semaphore_wait(
        barrier, chips + has_prev.astype(jnp.int32) + has_next.astype(jnp.int32))

    def start_next(part):
        @pl.when(has_next)
        def _():
            to_next(part).start()

    def start_own(part):
        for m in range(chips - 1):
            @pl.when(others[m] > chip)
            def _():
                to_chip(part, m, SPAN).start()

        @pl.when(core == 0)
        def _():
            to_partner(part, SPAN).start()

    def start_prev(part):
        @pl.when(has_prev)
        def _():
            wait_slot(part, 0)
            for m in range(chips - 1):
                @pl.when(others[m] < chip)
                def _():
                    to_chip(part, m, 0).start()

            @pl.when(core == 1)
            def _():
                to_partner(part, 0).start()

    def pass_on(part):
        for m in range(chips - 1):
            @pl.when(jnp.logical_or(others[m] < chip, has_prev))
            def _():
                wait_slot(part, slot_at(others[m] * 2 + core, spot))
                forward(part, m).start()

    def gather(part):
        for m in range(chips - 1):
            @pl.when(jnp.logical_or(others[m] < chip, has_prev))
            def _():
                wait_slot(part, slot_at(others[m] * 2 + 1 - core, spot))

        @pl.when(jnp.logical_or(core == 1, has_prev))
        def _():
            wait_slot(part, slot_at(chip * 2 + 1 - core, spot))

    def finish(part):
        @pl.when(has_next)
        def _():
            to_next(part).wait_send()
        for m in range(chips - 1):
            @pl.when(jnp.logical_or(others[m] > chip, has_prev))
            def _():
                to_chip(part, m, SPAN).wait_send()

            @pl.when(jnp.logical_or(others[m] < chip, has_prev))
            def _():
                forward(part, m).wait_send()

        @pl.when(jnp.logical_or(core == 0, has_prev))
        def _():
            to_partner(part, SPAN).wait_send()

    scale = math.log2(math.e) / math.sqrt(HEAD_WIDTH)
    steps = group // PER_STEP

    def masks():
        own = seg[SPAN].astype(jnp.float32)
        cols = jnp.broadcast_to(own, (tok, tok))
        rows = jnp.transpose(cols)
        far = jnp.broadcast_to(seg[0].astype(jnp.float32), (tok, tok))
        tri = (lax.broadcasted_iota(jnp.int32, (tok, tok), 1)
               <= lax.broadcasted_iota(jnp.int32, (tok, tok), 0))
        key_seg = jnp.where(tri, cols, far)
        tri_bias[...] = jnp.where(key_seg == rows, 0.0, -BIG)
        row_neg[...] = jnp.where(rows == rows[0:1, :], 0.0, -BIG)
        for r in range(1, SPAN):
            col_bias[r - 1] = jnp.where(
                seg[r].astype(jnp.float32) == rows[0:1, :], 0.0, -BIG)

    def attend(h, first, last):
        def step(it, carry):
            tri = (lax.broadcasted_iota(jnp.int32, (tok, tok), 1)
                   <= lax.broadcasted_iota(jnp.int32, (tok, tok), 0))
            col = [pl.multiple_of((h * group + it * PER_STEP + g) * HEAD_WIDTH, HEAD_WIDTH)
                   for g in range(PER_STEP)]
            q = jnp.concatenate([q_buf[:, pl.ds(c, HEAD_WIDTH)] for c in col], 0)
            nt = (((1,), (1,)), ((), ()))

            def dots(a, b):
                return lax.dot_general(a, b, nt, preferred_element_type=jnp.float32)

            def tall(x):
                return jnp.concatenate([x] * PER_STEP, 0)

            k_mid = kv[1:SPAN, h, 0].reshape((SPAN - 1) * tok, HEAD_WIDTH)
            v_mid = kv[1:SPAN, h, 1].reshape((SPAN - 1) * tok, HEAD_WIDTH)
            s_mid = dots(q, k_mid)
            s_own = dots(q, kv[SPAN, h, 0])
            s_far = dots(q, kv[0, h, 0])
            tri2 = tall(tri)
            s_tri = jnp.where(tri2, s_own, s_far) + tall(tri_bias[...])
            neg = tall(row_neg[...])
            mids = [s_mid[:, r * tok:(r + 1) * tok] + col_bias[r] for r in range(SPAN - 1)]
            top = functools.reduce(jnp.maximum, mids)
            top = jnp.max(jnp.maximum(top + neg, s_tri), axis=1, keepdims=True)
            p_tri = jnp.exp2((s_tri - top) * scale)
            lift = top - neg
            p_mid = [jnp.exp2((s - lift) * scale) for s in mids]
            p_own = jnp.where(tri2, p_tri, 0.0).astype(jnp.bfloat16)
            p_far = jnp.where(tri2, 0.0, p_tri).astype(jnp.bfloat16)
            ones = jnp.ones(((SPAN + 1) * tok, HEAD_WIDTH), jnp.bfloat16)
            v_all = jnp.concatenate([jnp.concatenate([v_mid, kv[SPAN, h, 1], kv[0, h, 1]], 0), ones], 1)
            p_all = jnp.concatenate([p.astype(jnp.bfloat16) for p in p_mid] + [p_own, p_far], 1)
            out = jnp.dot(p_all, v_all, preferred_element_type=jnp.float32)
            out = (out[:, :HEAD_WIDTH] / out[:, HEAD_WIDTH:]).astype(o_hbm.dtype)
            for g in range(PER_STEP):
                o_hbm[:, pl.ds(col[g], HEAD_WIDTH)] = out[g * tok:(g + 1) * tok]
            return carry
        lax.fori_loop(first, last, step, 0, unroll=2)

    seg_in.wait()
    start_next(0)
    load_in(0, 0).wait()
    load_in(0, 1).wait()
    start_next(1)
    start_own(0)
    start_own(1)
    for h in range(1, heads):
        load_in(h, 0).wait()
        load_in(h, 1).wait()
        start_next(1 + h)
    for part in range(2, min(3, heads + 1)):
        start_own(part)
    start_prev(0)
    start_prev(1)
    if heads > 1:
        start_prev(2)
    pass_on(0)
    pass_on(1)
    for h in range(heads):
        part = h + 1
        if part + 2 <= heads:
            start_own(part + 2)
            start_prev(part + 2)
        if h == 0:
            gather(0)
            masks()
        gather(part)
        load_q(h).wait()
        attend(h, 0, steps // 2)
        if part + 1 <= heads:
            pass_on(part + 1)
        attend(h, steps // 2, steps)
    for part in range(heads + 1):
        finish(part)


def shards(count, cp_count, query_proj, key_proj, value_projection, segment_ids):
    tok = query_proj.shape[0]
    heads = key_proj.shape[1] // HEAD_WIDTH
    group = query_proj.shape[1] // key_proj.shape[1]
    return pl.pallas_call(
        functools.partial(kernel, count, cp_count, heads, group),
        out_shape=pltpu.VMEM(query_proj.shape, query_proj.dtype),
        in_specs=[pl.BlockSpec(memory_space=pltpu.HBM)] * 4,
        out_specs=pl.BlockSpec(memory_space=pltpu.VMEM),
        scratch_shapes=[
            pltpu.VMEM((SPAN + 1, heads, 2, tok, HEAD_WIDTH), key_proj.dtype),
            pltpu.VMEM((SPAN + 1, 1, tok), segment_ids.dtype),
            pltpu.VMEM(query_proj.shape, query_proj.dtype),
            pltpu.VMEM((tok, tok), jnp.float32),
            pltpu.VMEM((tok, tok), jnp.float32),
            pltpu.VMEM((SPAN - 1, 1, tok), jnp.float32),
            pltpu.SemaphoreType.DMA((heads + 1, SPAN)),
            pltpu.SemaphoreType.DMA((heads + 1, SPAN)),
            pltpu.SemaphoreType.DMA((2 * heads + 1,)),
            pltpu.SemaphoreType.DMA((heads,)),
            pltpu.SemaphoreType.DMA((heads,)),
        ],
        compiler_params=pltpu.CompilerParams(collective_id=0, vmem_limit_bytes=24*2**20, has_side_effects=True),
        name="window_attention",
    )(*[pltpu.with_memory_space_constraint(a, pltpu.HBM) for a in (query_proj, key_proj, value_projection, segment_ids.reshape(1, tok))])


def solution(mesh):
    cp_count = mesh.shape["cp"]
    count = mesh.shape["grp"] * cp_count
    spec = P(("grp", "cp"), None)
    return jax.shard_map(
        functools.partial(shards, count, cp_count),
        mesh=mesh,
        in_specs=(spec, spec, spec, P(("grp", "cp"))),
        out_specs=spec,
        check_vma=False,
    )
```

```python
import functools
import math

import jax
import jax.numpy as jnp
from jax import lax
from jax.experimental import pallas as pl
from jax.experimental.pallas import tpu as pltpu
from jax.sharding import PartitionSpec as P

HEAD_WIDTH = 128
SPAN = 8
SEG_ROWS = 16
BASE = 16
BIG = 1e30
MESH = pl.DeviceIdType.MESH
NEXT, ACROSS, RELAY, PAIR, SHARE, UP = 0, 1, 4, 5, 6, 9
SENDS = 12


def kernel(
    count, cp_count, heads, group,
    q_hbm, k_hbm, v_hbm, s_hbm, o_ref,
    kv, seg, q_buf, acc, top_a, tri_bias, pair_bias, row_neg, col_bias,
    send_sem, recv_sem, in_sem, q_sem,
):
    tok = q_buf.shape[0]
    flat = lax.axis_index("grp") * cp_count + lax.axis_index("cp")
    spot = lax.rem(flat, SPAN)
    base = flat - spot
    chip, core = spot // 2, lax.rem(spot, 2)
    mate = chip * 2 + 1 - core
    has_prev = flat >= SPAN
    has_next = flat + SPAN < count
    chips = [jnp.bitwise_xor(chip, m) for m in (1, 2, 3)]
    spots = [o * 2 + core for o in chips]
    modes = 'RGRR'
    parts = len(modes)
    cuts = [0, 1, 2, 3, 4]

    def dev(f):
        return (f // cp_count, lax.rem(f, cp_count))

    def slot_at(owner, place):
        return lax.rem(owner - place + SPAN, SPAN)

    mate_dev = dev(base + mate)
    next_dev, prev_dev = dev(flat + SPAN), dev(flat - SPAN)
    side_dev = [dev(base + t) for t in spots]
    low = [o < chip for o in chips]
    high = [o > chip for o in chips]
    there = [slot_at(spot, t) for t in spots]
    shared = [slot_at(t, mate) for t in spots]
    other = [slot_at(o * 2 + 1 - core, spot) for o in chips]
    here = [slot_at(s, spot) for s in spots]
    pair_slot = slot_at(mate, spot)
    pair_dst = slot_at(spot, mate)
    pair_src = jnp.where(core == 0, SPAN, 0)
    side_src = [jnp.where(x, 0, SPAN) for x in low]
    arrivals = [jnp.where(low[m], here[m], SPAN + 1 + m) for m in range(3)]
    early_dst = [jnp.where(low[m], SPAN + 1 + m, there[m]) for m in range(3)]
    x_relay = jnp.where(chips[0] < chips[1], slot_at(spots[0], spots[1]), SPAN + 3)
    y_relay = slot_at(spots[1], spots[0])

    def span_of(p):
        begin = SEG_ROWS + 2 * tok * cuts[p] if p else 0
        return pl.ds(begin, SEG_ROWS + 2 * tok * cuts[p + 1] - begin)

    def view(p, slot):
        return kv.at[slot, span_of(p)]

    def remote(h, src, dst, k, target):
        return pltpu.make_async_remote_copy(
            src_ref=view(h, src), dst_ref=view(h, dst),
            send_sem=send_sem.at[h, k], recv_sem=recv_sem.at[h, dst],
            device_id=target, device_id_type=MESH,
        )

    def wait_slot(h, slot):
        remote(h, SPAN, slot, 0, mate_dev).wait_recv()

    def key_rows(h, which):
        return pl.ds(SEG_ROWS + (2 * h + which) * tok, tok)

    def load_in(h, which):
        ref = (k_hbm, v_hbm)[which]
        return pltpu.make_async_copy(
            ref.at[:, h * HEAD_WIDTH:(h + 1) * HEAD_WIDTH], kv.at[SPAN, key_rows(h, which)],
            in_sem.at[2 * h + which])

    width = group * HEAD_WIDTH

    def load_q(h):
        return pltpu.make_async_copy(
            q_hbm.at[:, h * width:(h + 1) * width], q_buf.at[:, h * width:(h + 1) * width],
            q_sem.at[h])

    seg_in = pltpu.make_async_copy(s_hbm, seg, in_sem.at[2 * heads])
    seg_in.start()
    for h in range(heads):
        for which in range(2):
            load_in(h, which).start()

    barrier = pltpu.get_barrier_semaphore()

    def hello(target):
        pl.semaphore_signal(barrier, inc=1, device_id=target, device_id_type=MESH)

    for t in [mate_dev] + side_dev:
        hello(t)

    @pl.when(has_prev)
    def _():
        hello(prev_dev)

    @pl.when(has_next)
    def _():
        hello(next_dev)

    for h in range(heads):
        load_q(h).start()

    @pl.when(jnp.logical_not(has_prev))
    def _():
        kv[0] = jnp.full(kv.shape[1:], -1, kv.dtype)
        for m in range(3):
            @pl.when(high[m])
            def _():
                for p in range(parts):
                    if modes[p] == "G":
                        size = 2 * tok * (cuts[p + 1] - cuts[p]) + (0 if p else SEG_ROWS)
                        kv[here[m], span_of(p)] = jnp.full((size, HEAD_WIDTH), -1, kv.dtype)

    seg_in.wait()
    ids = seg[...]
    line = lax.broadcasted_iota(jnp.int32, (SEG_ROWS, tok), 0)
    kv[SPAN, 0:SEG_ROWS] = jnp.where(
        line == 0, ids // BASE, jnp.where(line == 1, ids % BASE, 0)
    ).astype(jnp.float32).astype(kv.dtype)

    pl.semaphore_wait(
        barrier, 4 + has_prev.astype(jnp.int32) + has_next.astype(jnp.int32))

    def to_next(h):
        return remote(h, SPAN, 0, NEXT, next_dev)

    def direct(h, m):
        if modes[h] == "G":
            return remote(h, SPAN, early_dst[m], ACROSS + m, side_dev[m])
        return remote(h, side_src[m], there[m], ACROSS + m, side_dev[m])

    def relay(h):
        if modes[h] == "G":
            return remote(h, arrivals[0], x_relay, RELAY, side_dev[1])
        return remote(h, here[1], y_relay, RELAY, side_dev[0])

    def to_mate(h):
        return remote(h, pair_src, pair_dst, PAIR, mate_dev)

    def share(h, m):
        return remote(h, here[m], shared[m], SHARE + m, mate_dev)

    def up(h, m):
        return remote(h, SPAN + 1 + m, here[m], UP + m, next_dev)

    def loaded(p):
        for h in range(cuts[p], cuts[p + 1]):
            load_in(h, 0).wait()
            load_in(h, 1).wait()

    def open_next(h):
        loaded(h)

        @pl.when(has_next)
        def _():
            to_next(h).start()

    def open_own(h):
        for m in range(3 if modes[h] == "H" else 2):
            if modes[h] == "G":
                direct(h, m).start()
            else:
                @pl.when(high[m])
                def _():
                    direct(h, m).start()

        @pl.when(core == 0)
        def _():
            to_mate(h).start()

    def open_prev(h):
        @pl.when(has_prev)
        def _():
            wait_slot(h, 0)
        if modes[h] != "G":
            for m in range(3 if modes[h] == "H" else 2):
                @pl.when(low[m])
                def _():
                    direct(h, m).start()

        @pl.when(core == 1)
        def _():
            to_mate(h).start()

    def near(h):
        if modes[h] == "G":
            for m in range(2):
                plane(h, m)
        else:
            for m in (1, 0):
                wait_slot(h, here[m])
                if m == 1 and modes[h] == "R":
                    relay(h).start()
                share(h, m).start()

    def far(h):
        if modes[h] == "G":
            plane(h, 2)
        else:
            wait_slot(h, here[2])
            share(h, 2).start()

    def plane(h, m):
        wait_slot(h, arrivals[m])
        if m == 0:
            relay(h).start()

        @pl.when(jnp.logical_and(high[m], has_next))
        def _():
            up(h, m).start()

        @pl.when(low[m])
        def _():
            share(h, m).start()

    def settle(h, m):
        @pl.when(high[m])
        def _():
            @pl.when(has_prev)
            def _():
                wait_slot(h, here[m])
            share(h, m).start()

    def ready_pair(h):
        wait_slot(h, pair_slot)

    def finish(h):
        @pl.when(has_next)
        def _():
            to_next(h).wait_send()
        for m in range(3 if modes[h] == "H" else 2):
            direct(h, m).wait_send()
        if modes[h] != "H":
            relay(h).wait_send()
        to_mate(h).wait_send()
        for m in range(3):
            share(h, m).wait_send()
            if modes[h] == "G":
                @pl.when(jnp.logical_and(high[m], has_next))
                def _():
                    up(h, m).wait_send()

    scale = math.log2(math.e) / math.sqrt(HEAD_WIDTH)

    def ids_of(slot):
        rows = kv[slot, 0:SEG_ROWS].astype(jnp.float32)
        return rows[0:1] * BASE + rows[1:2]

    def lower():
        return (lax.broadcasted_iota(jnp.int32, (tok, tok), 1)
                <= lax.broadcasted_iota(jnp.int32, (tok, tok), 0))

    def masks_a():
        cols = jnp.broadcast_to(ids_of(SPAN), (tok, tok))
        rows = jnp.transpose(cols)
        old = jnp.broadcast_to(ids_of(0), (tok, tok))
        tri_bias[...] = jnp.where(jnp.where(lower(), cols, old) == rows, 0.0, -BIG)
        pair_bias[...] = jnp.where(jnp.broadcast_to(ids_of(pair_slot), (tok, tok)) == rows, 0.0, -BIG)
        row_neg[...] = jnp.where(rows == rows[0:1, :], 0.0, -BIG)

    def dots(a, b):
        return lax.dot_general(a, b, (((1,), (1,)), ((), ())), preferred_element_type=jnp.float32)

    def queries(c, n):
        return jnp.concatenate(
            [q_buf[:, (c + g) * HEAD_WIDTH:(c + g + 1) * HEAD_WIDTH] for g in range(n)], 0)

    def part_a(h):
        tall = lambda x: jnp.concatenate([x] * group, 0)
        q = queries(h * group, group)
        tri2 = tall(lower())
        s_own = dots(q, kv[SPAN, key_rows(h, 0)])
        s_old = dots(q, kv[0, key_rows(h, 0)])
        s_pair = dots(q, kv[pair_slot, key_rows(h, 0)]) + tall(pair_bias[...])
        s_tri = jnp.where(tri2, s_own, s_old) + tall(tri_bias[...])
        top = jnp.max(jnp.maximum(s_tri, s_pair), axis=1, keepdims=True)
        p_tri = jnp.exp2((s_tri - top) * scale)
        p_pair = jnp.exp2((s_pair - top) * scale).astype(jnp.bfloat16)
        p_own = jnp.where(tri2, p_tri, 0.0).astype(jnp.bfloat16)
        p_old = jnp.where(tri2, 0.0, p_tri).astype(jnp.bfloat16)
        v_all = jnp.concatenate([kv[SPAN, key_rows(h, 1)], kv[0, key_rows(h, 1)],
                                 kv[pair_slot, key_rows(h, 1)]], 0)
        ones = jnp.ones((3 * tok, HEAD_WIDTH), jnp.bfloat16)
        out = jnp.dot(jnp.concatenate([p_own, p_old, p_pair], 1),
                      jnp.concatenate([v_all, ones], 1), preferred_element_type=jnp.float32)
        acc[h * group:(h + 1) * group] = out.reshape(group, tok, 2 * HEAD_WIDTH)
        top_a[h * group:(h + 1) * group] = jnp.broadcast_to(
            top, (group * tok, HEAD_WIDTH)).reshape(group, tok, HEAD_WIDTH)

    def part_b(h, starts, last, n=0, k=1):
        size = group // k
        c = h * group + n * size
        wide = 2 * len(starts) * tok
        tall = lambda x: jnp.concatenate([x] * size, 0)

        def gather(which):
            return jnp.concatenate(
                [kv[pl.ds(e, 2), key_rows(h, which)].reshape(2 * tok, HEAD_WIDTH) for e in starts], 0)

        s_mid = dots(queries(c, size), gather(0))
        neg = tall(row_neg[...])
        bias = [col_bias[e + r] for e in starts for r in range(2)]
        mids = [s_mid[:, r * tok:(r + 1) * tok] + b for r, b in enumerate(bias)]
        old = top_a[c:c + size].reshape(size * tok, HEAD_WIDTH)
        top = jnp.max(functools.reduce(jnp.maximum, mids) + neg, axis=1, keepdims=True)
        top = jnp.maximum(old, top)
        fade = jnp.exp2((old - top) * scale)
        lift = top - neg
        p_mid = [jnp.exp2((s - lift) * scale).astype(jnp.bfloat16) for s in mids]
        ones = jnp.ones((wide, HEAD_WIDTH), jnp.bfloat16)
        out = jnp.dot(jnp.concatenate(p_mid, 1), jnp.concatenate([gather(1), ones], 1),
                      preferred_element_type=jnp.float32)
        was = acc[c:c + size].reshape(size * tok, 2 * HEAD_WIDTH)
        value = out[:, :HEAD_WIDTH] + fade * was[:, :HEAD_WIDTH]
        total = out[:, HEAD_WIDTH:] + fade * was[:, HEAD_WIDTH:]
        if last:
            out = (value / total).astype(o_ref.dtype)
            for g in range(size):
                o_ref[:, (c + g) * HEAD_WIDTH:(c + g + 1) * HEAD_WIDTH] = out[g * tok:(g + 1) * tok]
        else:
            acc[c:c + size] = jnp.concatenate([value, total], 1).reshape(size, tok, 2 * HEAD_WIDTH)
            top_a[c:c + size] = top.reshape(size, tok, HEAD_WIDTH)

    pairs = [slot_at(o * 2, spot) for o in chips]

    def masks_b(which):
        head = jnp.broadcast_to(ids_of(SPAN)[:, 0:1], (1, tok))
        for m in which:
            for r in range(2):
                col_bias[pairs[m] + r] = jnp.where(ids_of(pairs[m] + r) == head, 0.0, -BIG)

    def take(p, m):
        if modes[p] == "G":
            plane(p, m)
        else:
            wait_slot(p, here[m])
            if m == 1 and modes[p] == "R":
                relay(p).start()
            share(p, m).start()

    def do_a(p):
        ready_pair(p)
        load_q(p).wait()
        if p == 0:
            masks_a()
        part_a(p)

    def do_near(p):
        for m in range(2):
            wait_slot(p, other[m])
        if p == 0:
            masks_b((0, 1))
        part_b(p, pairs[:2], False)

    def do_far(p):
        wait_slot(p, other[2])
        if p == 0:
            masks_b((2,))
        part_b(p, pairs[2:], True)

    open_next(0)
    open_own(0)
    open_next(2)
    open_own(2)
    open_next(3)
    open_own(3)
    open_next(1)
    open_own(1)
    open_prev(0)
    open_prev(2)
    do_a(0)
    open_prev(3)
    do_a(2)
    take(1,0)
    take(0,1)
    take(2,0)
    open_prev(1)
    take(1,1)
    take(0,0)
    take(2,1)
    do_a(3)
    take(3,1)
    take(3,0)
    do_a(1)
    do_near(0)
    take(1,2)
    take(0,2)
    do_near(2)
    settle(1,0)
    settle(1,1)
    take(2,2)
    do_far(0)
    do_near(3)
    settle(1,2)
    take(3,2)
    do_near(1)
    do_far(2)
    do_far(3)
    do_far(1)
    for p in range(4):
        finish(p)


def shards(count, cp_count, query_proj, key_proj, value_projection, segment_ids):
    tok = query_proj.shape[0]
    heads = key_proj.shape[1] // HEAD_WIDTH
    group = query_proj.shape[1] // key_proj.shape[1]
    inputs = (query_proj, key_proj, value_projection, segment_ids.reshape(1, tok))
    return pl.pallas_call(
        functools.partial(kernel, count, cp_count, heads, group),
        out_shape=pltpu.VMEM(query_proj.shape, query_proj.dtype),
        in_specs=[pl.BlockSpec(memory_space=pl.ANY)] * 4,
        out_specs=pl.BlockSpec(memory_space=pltpu.VMEM),
        scratch_shapes=[
            pltpu.VMEM((SPAN + 4, SEG_ROWS + 2 * heads * tok, HEAD_WIDTH), key_proj.dtype),
            pltpu.VMEM((1, tok), segment_ids.dtype),
            pltpu.VMEM(query_proj.shape, query_proj.dtype),
            pltpu.VMEM((heads * group, tok, 2 * HEAD_WIDTH), jnp.float32),
            pltpu.VMEM((heads * group, tok, HEAD_WIDTH), jnp.float32),
            pltpu.VMEM((tok, tok), jnp.float32),
            pltpu.VMEM((tok, tok), jnp.float32),
            pltpu.VMEM((tok, tok), jnp.float32),
            pltpu.VMEM((SPAN, 1, tok), jnp.float32),
            pltpu.SemaphoreType.DMA((4, SENDS)),
            pltpu.SemaphoreType.DMA((4, SPAN + 4)),
            pltpu.SemaphoreType.DMA((2 * heads + 1,)),
            pltpu.SemaphoreType.DMA((heads,)),
        ],
        compiler_params=pltpu.CompilerParams(
            collective_id=0, has_side_effects=True, vmem_limit_bytes=24 * 2**20),
        name="window_attention",
    )(*[pltpu.with_memory_space_constraint(x, pltpu.HBM) for x in inputs])


def solution(mesh):
    cp_count = mesh.shape["cp"]
    count = mesh.shape["grp"] * cp_count
    spec = P(("grp", "cp"), None)
    return jax.shard_map(
        functools.partial(shards, count, cp_count),
        mesh=mesh,
        in_specs=(spec, spec, spec, P(("grp", "cp"))),
        out_specs=spec,
        check_vma=False,
    )
```

```python
import functools
import math

import jax
import jax.numpy as jnp
from jax import lax
from jax.experimental import pallas as pl
from jax.experimental.pallas import tpu as pltpu
from jax.sharding import PartitionSpec as P

HEAD_WIDTH = 128
SPAN = 8
SEG_ROWS = 16
BASE = 16
BIG = 1e30
MESH = pl.DeviceIdType.MESH
NEXT, ACROSS, RELAY, PAIR, SHARE, UP = 0, 1, 4, 5, 6, 9
SENDS = 12


def kernel(
    count, cp_count, heads, group,
    q_hbm, k_hbm, v_hbm, s_hbm, o_ref,
    kv, seg, q_buf, acc, top_a, tri_bias, pair_bias, row_neg, col_bias,
    send_sem, recv_sem, in_sem, q_sem,
):
    tok = q_buf.shape[0]
    flat = lax.axis_index("grp") * cp_count + lax.axis_index("cp")
    spot = lax.rem(flat, SPAN)
    base = flat - spot
    chip, core = spot // 2, lax.rem(spot, 2)
    mate = chip * 2 + 1 - core
    has_prev = flat >= SPAN
    has_next = flat + SPAN < count
    chips = [jnp.bitwise_xor(chip, m) for m in (1, 2, 3)]
    spots = [o * 2 + core for o in chips]
    modes = 'RGRR'
    parts = len(modes)
    cuts = [0, 1, 2, 3, 4]

    def dev(f):
        return (f // cp_count, lax.rem(f, cp_count))

    def slot_at(owner, place):
        return lax.rem(owner - place + SPAN, SPAN)

    mate_dev = dev(base + mate)
    next_dev, prev_dev = dev(flat + SPAN), dev(flat - SPAN)
    side_dev = [dev(base + t) for t in spots]
    low = [o < chip for o in chips]
    high = [o > chip for o in chips]
    there = [slot_at(spot, t) for t in spots]
    shared = [slot_at(t, mate) for t in spots]
    other = [slot_at(o * 2 + 1 - core, spot) for o in chips]
    here = [slot_at(s, spot) for s in spots]
    pair_slot = slot_at(mate, spot)
    pair_dst = slot_at(spot, mate)
    pair_src = jnp.where(core == 0, SPAN, 0)
    side_src = [jnp.where(x, 0, SPAN) for x in low]
    arrivals = [jnp.where(low[m], here[m], SPAN + 1 + m) for m in range(3)]
    early_dst = [jnp.where(low[m], SPAN + 1 + m, there[m]) for m in range(3)]
    x_relay = jnp.where(chips[0] < chips[1], slot_at(spots[0], spots[1]), SPAN + 3)
    y_relay = slot_at(spots[1], spots[0])

    def span_of(p):
        begin = SEG_ROWS + 2 * tok * cuts[p] if p else 0
        return pl.ds(begin, SEG_ROWS + 2 * tok * cuts[p + 1] - begin)

    def view(p, slot):
        return kv.at[slot, span_of(p)]

    def remote(h, src, dst, k, target):
        return pltpu.make_async_remote_copy(
            src_ref=view(h, src), dst_ref=view(h, dst),
            send_sem=send_sem.at[h, k], recv_sem=recv_sem.at[h, dst],
            device_id=target, device_id_type=MESH,
        )

    def wait_slot(h, slot):
        remote(h, SPAN, slot, 0, mate_dev).wait_recv()

    def key_rows(h, which):
        return pl.ds(SEG_ROWS + (2 * h + which) * tok, tok)

    def load_in(h, which):
        ref = (k_hbm, v_hbm)[which]
        return pltpu.make_async_copy(
            ref.at[:, h * HEAD_WIDTH:(h + 1) * HEAD_WIDTH], kv.at[SPAN, key_rows(h, which)],
            in_sem.at[2 * h + which])

    width = group * HEAD_WIDTH

    def load_q(h):
        return pltpu.make_async_copy(
            q_hbm.at[:, h * width:(h + 1) * width], q_buf.at[:, h * width:(h + 1) * width],
            q_sem.at[h])

    seg_in = pltpu.make_async_copy(s_hbm, seg, in_sem.at[2 * heads])
    seg_in.start()
    for h in range(heads):
        for which in range(2):
            load_in(h, which).start()

    barrier = pltpu.get_barrier_semaphore()

    def hello(target):
        pl.semaphore_signal(barrier, inc=1, device_id=target, device_id_type=MESH)

    for t in [mate_dev] + side_dev:
        hello(t)

    @pl.when(has_prev)
    def _():
        hello(prev_dev)

    @pl.when(has_next)
    def _():
        hello(next_dev)

    for h in range(heads):
        load_q(h).start()

    @pl.when(jnp.logical_not(has_prev))
    def _():
        kv[0] = jnp.full(kv.shape[1:], -1, kv.dtype)
        for m in range(3):
            @pl.when(high[m])
            def _():
                kv[here[m]] = jnp.full(kv.shape[1:], -1, kv.dtype)

    seg_in.wait()
    ids = seg[...]
    line = lax.broadcasted_iota(jnp.int32, (SEG_ROWS, tok), 0)
    kv[SPAN, 0:SEG_ROWS] = jnp.where(
        line == 0, ids // BASE, jnp.where(line == 1, ids % BASE, 0)
    ).astype(jnp.float32).astype(kv.dtype)

    pl.semaphore_wait(
        barrier, 4 + has_prev.astype(jnp.int32) + has_next.astype(jnp.int32))

    def to_next(h):
        return remote(h, SPAN, 0, NEXT, next_dev)

    def direct(h, m):
        if modes[h] == "G":
            return remote(h, SPAN, early_dst[m], ACROSS + m, side_dev[m])
        return remote(h, side_src[m], there[m], ACROSS + m, side_dev[m])

    def relay(h):
        if modes[h] == "G":
            return remote(h, arrivals[0], x_relay, RELAY, side_dev[1])
        return remote(h, here[1], y_relay, RELAY, side_dev[0])

    def to_mate(h):
        return remote(h, pair_src, pair_dst, PAIR, mate_dev)

    def share(h, m):
        return remote(h, here[m], shared[m], SHARE + m, mate_dev)

    def up(h, m):
        return remote(h, SPAN + 1 + m, here[m], UP + m, next_dev)

    def loaded(p):
        for h in range(cuts[p], cuts[p + 1]):
            load_in(h, 0).wait()
            load_in(h, 1).wait()

    def open_next(h):
        loaded(h)

        @pl.when(has_next)
        def _():
            to_next(h).start()

    def open_own(h):
        for m in range(2):
            if modes[h] == "G":
                direct(h, m).start()
            else:
                @pl.when(high[m])
                def _():
                    direct(h, m).start()

        @pl.when(core == 0)
        def _():
            to_mate(h).start()

    def open_prev(h):
        @pl.when(has_prev)
        def _():
            wait_slot(h, 0)
            if modes[h] != "G":
                for m in range(2):
                    @pl.when(low[m])
                    def _():
                        direct(h, m).start()

        @pl.when(core == 1)
        def _():
            to_mate(h).start()

    def plane(h, m):
        wait_slot(h, arrivals[m])
        if m == 0:
            relay(h).start()

        @pl.when(jnp.logical_and(high[m], has_next))
        def _():
            up(h, m).start()

        @pl.when(low[m])
        def _():
            share(h, m).start()

    def settle(h, m):
        @pl.when(high[m])
        def _():
            @pl.when(has_prev)
            def _():
                wait_slot(h, here[m])
            share(h, m).start()

    def ready_pair(h):
        wait_slot(h, pair_slot)

    def finish(h):
        @pl.when(has_next)
        def _():
            to_next(h).wait_send()
        if modes[h] == "G":
            for m in range(2):
                direct(h, m).wait_send()
            relay(h).wait_send()
        else:
            for m in range(2):
                @pl.when(jnp.logical_or(high[m], has_prev))
                def _():
                    direct(h, m).wait_send()

            @pl.when(jnp.logical_or(low[1], has_prev))
            def _():
                relay(h).wait_send()
        to_mate(h).wait_send()
        for m in range(3):
            share(h, m).wait_send()
            if modes[h] == "G":
                @pl.when(jnp.logical_and(high[m], has_next))
                def _():
                    up(h, m).wait_send()

    scale = math.log2(math.e) / math.sqrt(HEAD_WIDTH)

    def ids_of(slot):
        rows = kv[slot, 0:SEG_ROWS].astype(jnp.float32)
        return rows[0:1] * BASE + rows[1:2]

    def lower():
        return (lax.broadcasted_iota(jnp.int32, (tok, tok), 1)
                <= lax.broadcasted_iota(jnp.int32, (tok, tok), 0))

    def masks_a():
        cols = jnp.broadcast_to(ids_of(SPAN), (tok, tok))
        rows = jnp.transpose(cols)
        old = jnp.broadcast_to(ids_of(0), (tok, tok))
        tri_bias[...] = jnp.where(jnp.where(lower(), cols, old) == rows, 0.0, -BIG)
        pair_bias[...] = jnp.where(jnp.broadcast_to(ids_of(pair_slot), (tok, tok)) == rows, 0.0, -BIG)
        row_neg[...] = jnp.where(rows == rows[0:1, :], 0.0, -BIG)

    def dots(a, b):
        return lax.dot_general(a, b, (((1,), (1,)), ((), ())), preferred_element_type=jnp.float32)

    def queries(c, n):
        return jnp.concatenate(
            [q_buf[:, (c + g) * HEAD_WIDTH:(c + g + 1) * HEAD_WIDTH] for g in range(n)], 0)

    def part_a(h):
        tall = lambda x: jnp.concatenate([x] * group, 0)
        q = queries(h * group, group)
        tri2 = tall(lower())
        s_own = dots(q, kv[SPAN, key_rows(h, 0)])
        s_old = dots(q, kv[0, key_rows(h, 0)])
        s_pair = dots(q, kv[pair_slot, key_rows(h, 0)]) + tall(pair_bias[...])
        s_tri = jnp.where(tri2, s_own, s_old) + tall(tri_bias[...])
        top = jnp.max(jnp.maximum(s_tri, s_pair), axis=1, keepdims=True)
        p_tri = jnp.exp2((s_tri - top) * scale)
        p_pair = jnp.exp2((s_pair - top) * scale).astype(jnp.bfloat16)
        p_own = jnp.where(tri2, p_tri, 0.0).astype(jnp.bfloat16)
        p_old = jnp.where(tri2, 0.0, p_tri).astype(jnp.bfloat16)
        v_all = jnp.concatenate([kv[SPAN, key_rows(h, 1)], kv[0, key_rows(h, 1)],
                                 kv[pair_slot, key_rows(h, 1)]], 0)
        ones = jnp.ones((3 * tok, HEAD_WIDTH), jnp.bfloat16)
        out = jnp.dot(jnp.concatenate([p_own, p_old, p_pair], 1),
                      jnp.concatenate([v_all, ones], 1), preferred_element_type=jnp.float32)
        acc[h * group:(h + 1) * group] = out.reshape(group, tok, 2 * HEAD_WIDTH)
        top_a[h * group:(h + 1) * group] = jnp.broadcast_to(
            top, (group * tok, HEAD_WIDTH)).reshape(group, tok, HEAD_WIDTH)

    def part_b(h, starts, last, n=0, k=1):
        size = group // k
        c = h * group + n * size
        wide = 2 * len(starts) * tok
        tall = lambda x: jnp.concatenate([x] * size, 0)

        def gather(which):
            return jnp.concatenate(
                [kv[pl.ds(e, 2), key_rows(h, which)].reshape(2 * tok, HEAD_WIDTH) for e in starts], 0)

        s_mid = dots(queries(c, size), gather(0))
        neg = tall(row_neg[...])
        bias = [col_bias[e + r] for e in starts for r in range(2)]
        mids = [s_mid[:, r * tok:(r + 1) * tok] + b for r, b in enumerate(bias)]
        old = top_a[c:c + size].reshape(size * tok, HEAD_WIDTH)
        top = jnp.max(functools.reduce(jnp.maximum, mids) + neg, axis=1, keepdims=True)
        top = jnp.maximum(old, top)
        fade = jnp.exp2((old - top) * scale)
        lift = top - neg
        p_mid = [jnp.exp2((s - lift) * scale).astype(jnp.bfloat16) for s in mids]
        ones = jnp.ones((wide, HEAD_WIDTH), jnp.bfloat16)
        out = jnp.dot(jnp.concatenate(p_mid, 1), jnp.concatenate([gather(1), ones], 1),
                      preferred_element_type=jnp.float32)
        was = acc[c:c + size].reshape(size * tok, 2 * HEAD_WIDTH)
        value = out[:, :HEAD_WIDTH] + fade * was[:, :HEAD_WIDTH]
        total = out[:, HEAD_WIDTH:] + fade * was[:, HEAD_WIDTH:]
        if last:
            out = (value / total).astype(o_ref.dtype)
            for g in range(size):
                o_ref[:, (c + g) * HEAD_WIDTH:(c + g + 1) * HEAD_WIDTH] = out[g * tok:(g + 1) * tok]
        else:
            acc[c:c + size] = jnp.concatenate([value, total], 1).reshape(size, tok, 2 * HEAD_WIDTH)
            top_a[c:c + size] = top.reshape(size, tok, HEAD_WIDTH)

    pairs = [slot_at(o * 2, spot) for o in chips]

    def masks_b(which):
        head = jnp.broadcast_to(ids_of(SPAN)[:, 0:1], (1, tok))
        for m in which:
            for r in range(2):
                col_bias[pairs[m] + r] = jnp.where(ids_of(pairs[m] + r) == head, 0.0, -BIG)

    def take(p, m):
        if modes[p] == "G":
            plane(p, m)
        else:
            @pl.when(jnp.logical_or(low[m], has_prev))
            def _():
                wait_slot(p, here[m])
                if m == 1:
                    relay(p).start()
            share(p, m).start()

    def do_a(p):
        ready_pair(p)
        load_q(p).wait()
        if p == 0:
            masks_a()
        part_a(p)

    def do_near(p):
        for m in range(2):
            wait_slot(p, other[m])
        if p == 0:
            masks_b((0, 1))
        part_b(p, pairs[:2], False)

    def do_far(p):
        wait_slot(p, other[2])
        if p == 0:
            masks_b((2,))
        part_b(p, pairs[2:], True)

    open_next(0)
    open_own(0)
    open_next(2)
    open_own(2)
    open_next(3)
    open_own(3)
    open_next(1)
    open_own(1)
    open_prev(0)
    open_prev(2)
    do_a(0)
    open_prev(3)
    do_a(2)
    take(1,0)
    take(0,1)
    take(2,0)
    open_prev(1)
    take(1,1)
    take(0,0)
    take(2,1)
    do_a(3)
    take(3,1)
    take(3,0)
    do_a(1)
    do_near(0)
    take(1,2)
    take(0,2)
    do_near(2)
    settle(1,0)
    settle(1,1)
    take(2,2)
    do_near(3)
    take(3,2)
    do_far(0)
    settle(1,2)
    do_near(1)
    do_far(2)
    do_far(1)
    do_far(3)
    for p in range(4):
        finish(p)


def shards(count, cp_count, query_proj, key_proj, value_projection, segment_ids):
    tok = query_proj.shape[0]
    heads = key_proj.shape[1] // HEAD_WIDTH
    group = query_proj.shape[1] // key_proj.shape[1]
    inputs = (query_proj, key_proj, value_projection, segment_ids.reshape(1, tok))
    return pl.pallas_call(
        functools.partial(kernel, count, cp_count, heads, group),
        out_shape=pltpu.VMEM(query_proj.shape, query_proj.dtype),
        in_specs=[pl.BlockSpec(memory_space=pl.ANY)] * 4,
        out_specs=pl.BlockSpec(memory_space=pltpu.VMEM),
        scratch_shapes=[
            pltpu.VMEM((SPAN + 4, SEG_ROWS + 2 * heads * tok, HEAD_WIDTH), key_proj.dtype),
            pltpu.VMEM((1, tok), segment_ids.dtype),
            pltpu.VMEM(query_proj.shape, query_proj.dtype),
            pltpu.VMEM((heads * group, tok, 2 * HEAD_WIDTH), jnp.float32),
            pltpu.VMEM((heads * group, tok, HEAD_WIDTH), jnp.float32),
            pltpu.VMEM((tok, tok), jnp.float32),
            pltpu.VMEM((tok, tok), jnp.float32),
            pltpu.VMEM((tok, tok), jnp.float32),
            pltpu.VMEM((SPAN, 1, tok), jnp.float32),
            pltpu.SemaphoreType.DMA((4, SENDS)),
            pltpu.SemaphoreType.DMA((4, SPAN + 4)),
            pltpu.SemaphoreType.DMA((2 * heads + 1,)),
            pltpu.SemaphoreType.DMA((heads,)),
        ],
        compiler_params=pltpu.CompilerParams(
            collective_id=0, has_side_effects=True, vmem_limit_bytes=24 * 2**20),
        name="window_attention",
    )(*[pltpu.with_memory_space_constraint(x, pltpu.HBM) for x in inputs])


def solution(mesh):
    cp_count = mesh.shape["cp"]
    count = mesh.shape["grp"] * cp_count
    spec = P(("grp", "cp"), None)
    return jax.shard_map(
        functools.partial(shards, count, cp_count),
        mesh=mesh,
        in_specs=(spec, spec, spec, P(("grp", "cp"))),
        out_specs=spec,
        check_vma=False,
    )
```

```python
import functools
import math

import jax
import jax.numpy as jnp
from jax import lax
from jax.experimental import pallas as pl
from jax.experimental.pallas import tpu as pltpu
from jax.sharding import PartitionSpec as P

HEAD_WIDTH = 128
SPAN = 8
SEG_ROWS = 16
BASE = 16
BIG = 1e30
MESH = pl.DeviceIdType.MESH
NEXT, ACROSS, RELAY, PAIR, SHARE, UP = 0, 1, 4, 5, 6, 9
SENDS = 12


def kernel(
    count, cp_count, heads, group,
    q_hbm, k_hbm, v_hbm, s_hbm, o_ref,
    kv, seg, q_buf, acc, top_a, tri_bias, pair_bias, row_neg, col_bias,
    send_sem, recv_sem, in_sem, q_sem,
):
    tok = q_buf.shape[0]
    flat = lax.axis_index("grp") * cp_count + lax.axis_index("cp")
    spot = lax.rem(flat, SPAN)
    base = flat - spot
    chip, core = spot // 2, lax.rem(spot, 2)
    mate = chip * 2 + 1 - core
    has_prev = flat >= SPAN
    has_next = flat + SPAN < count
    chips = [jnp.bitwise_xor(chip, m) for m in (1, 2, 3)]
    spots = [o * 2 + core for o in chips]
    modes = 'RGRR'
    parts = len(modes)
    cuts = [0, 1, 2, 3, 4]

    def dev(f):
        return (f // cp_count, lax.rem(f, cp_count))

    def slot_at(owner, place):
        return lax.rem(owner - place + SPAN, SPAN)

    mate_dev = dev(base + mate)
    next_dev, prev_dev = dev(flat + SPAN), dev(flat - SPAN)
    side_dev = [dev(base + t) for t in spots]
    low = [o < chip for o in chips]
    high = [o > chip for o in chips]
    there = [slot_at(spot, t) for t in spots]
    shared = [slot_at(t, mate) for t in spots]
    other = [slot_at(o * 2 + 1 - core, spot) for o in chips]
    here = [slot_at(s, spot) for s in spots]
    pair_slot = slot_at(mate, spot)
    pair_dst = slot_at(spot, mate)
    pair_src = jnp.where(core == 0, SPAN, 0)
    side_src = [jnp.where(x, 0, SPAN) for x in low]
    arrivals = [jnp.where(low[m], here[m], SPAN + 1 + m) for m in range(3)]
    early_dst = [jnp.where(low[m], SPAN + 1 + m, there[m]) for m in range(3)]
    x_relay = jnp.where(chips[0] < chips[1], slot_at(spots[0], spots[1]), SPAN + 3)
    y_relay = slot_at(spots[1], spots[0])

    def span_of(p):
        begin = SEG_ROWS + 2 * tok * cuts[p] if p else 0
        return pl.ds(begin, SEG_ROWS + 2 * tok * cuts[p + 1] - begin)

    def view(p, slot):
        return kv.at[slot, span_of(p)]

    def remote(h, src, dst, k, target):
        return pltpu.make_async_remote_copy(
            src_ref=view(h, src), dst_ref=view(h, dst),
            send_sem=send_sem.at[h, k], recv_sem=recv_sem.at[h, dst],
            device_id=target, device_id_type=MESH,
        )

    def wait_slot(h, slot):
        remote(h, SPAN, slot, 0, mate_dev).wait_recv()

    def key_rows(h, which):
        return pl.ds(SEG_ROWS + (2 * h + which) * tok, tok)

    def load_in(h, which):
        ref = (k_hbm, v_hbm)[which]
        return pltpu.make_async_copy(
            ref.at[:, h * HEAD_WIDTH:(h + 1) * HEAD_WIDTH], kv.at[SPAN, key_rows(h, which)],
            in_sem.at[2 * h + which])

    width = group * HEAD_WIDTH

    def load_q(h):
        return pltpu.make_async_copy(
            q_hbm.at[:, h * width:(h + 1) * width], q_buf.at[:, h * width:(h + 1) * width],
            q_sem.at[h])

    seg_in = pltpu.make_async_copy(s_hbm, seg, in_sem.at[2 * heads])
    seg_in.start()
    for h in range(heads):
        for which in range(2):
            load_in(h, which).start()

    barrier = pltpu.get_barrier_semaphore()

    def hello(target):
        pl.semaphore_signal(barrier, inc=1, device_id=target, device_id_type=MESH)

    for t in [mate_dev] + side_dev:
        hello(t)

    @pl.when(has_prev)
    def _():
        hello(prev_dev)

    @pl.when(has_next)
    def _():
        hello(next_dev)

    for h in range(heads):
        load_q(h).start()

    @pl.when(jnp.logical_not(has_prev))
    def _():
        kv[0] = jnp.full(kv.shape[1:], -1, kv.dtype)
        for m in range(3):
            @pl.when(high[m])
            def _():
                kv[here[m]] = jnp.full(kv.shape[1:], -1, kv.dtype)

    seg_in.wait()
    ids = seg[...]
    line = lax.broadcasted_iota(jnp.int32, (SEG_ROWS, tok), 0)
    kv[SPAN, 0:SEG_ROWS] = jnp.where(
        line == 0, ids // BASE, jnp.where(line == 1, ids % BASE, 0)
    ).astype(jnp.float32).astype(kv.dtype)

    pl.semaphore_wait(
        barrier, 4 + has_prev.astype(jnp.int32) + has_next.astype(jnp.int32))

    def to_next(h):
        return remote(h, SPAN, 0, NEXT, next_dev)

    def direct(h, m):
        if modes[h] == "G":
            return remote(h, SPAN, early_dst[m], ACROSS + m, side_dev[m])
        return remote(h, side_src[m], there[m], ACROSS + m, side_dev[m])

    def relay(h):
        if modes[h] == "G":
            return remote(h, arrivals[0], x_relay, RELAY, side_dev[1])
        return remote(h, here[1], y_relay, RELAY, side_dev[0])

    def to_mate(h):
        return remote(h, pair_src, pair_dst, PAIR, mate_dev)

    def share(h, m):
        return remote(h, here[m], shared[m], SHARE + m, mate_dev)

    def up(h, m):
        return remote(h, SPAN + 1 + m, here[m], UP + m, next_dev)

    def loaded(p):
        for h in range(cuts[p], cuts[p + 1]):
            load_in(h, 0).wait()
            load_in(h, 1).wait()

    def open_next(h):
        loaded(h)

        @pl.when(has_next)
        def _():
            to_next(h).start()

    def open_own(h):
        for m in range(2):
            if modes[h] == "G":
                direct(h, m).start()
            else:
                @pl.when(high[m])
                def _():
                    direct(h, m).start()

        @pl.when(core == 0)
        def _():
            to_mate(h).start()

    def open_prev(h):
        @pl.when(has_prev)
        def _():
            wait_slot(h, 0)
            if modes[h] != "G":
                for m in range(2):
                    @pl.when(low[m])
                    def _():
                        direct(h, m).start()

        @pl.when(core == 1)
        def _():
            to_mate(h).start()

    def plane(h, m):
        wait_slot(h, arrivals[m])
        if m == 0:
            relay(h).start()

        @pl.when(jnp.logical_and(high[m], has_next))
        def _():
            up(h, m).start()

        @pl.when(low[m])
        def _():
            share(h, m).start()

    def settle(h, m):
        @pl.when(high[m])
        def _():
            @pl.when(has_prev)
            def _():
                wait_slot(h, here[m])
            share(h, m).start()

    def ready_pair(h):
        wait_slot(h, pair_slot)

    def finish(h):
        @pl.when(has_next)
        def _():
            to_next(h).wait_send()
        if modes[h] == "G":
            for m in range(2):
                direct(h, m).wait_send()
            relay(h).wait_send()
        else:
            for m in range(2):
                @pl.when(jnp.logical_or(high[m], has_prev))
                def _():
                    direct(h, m).wait_send()

            @pl.when(jnp.logical_or(low[1], has_prev))
            def _():
                relay(h).wait_send()
        to_mate(h).wait_send()
        for m in range(3):
            share(h, m).wait_send()
            if modes[h] == "G":
                @pl.when(jnp.logical_and(high[m], has_next))
                def _():
                    up(h, m).wait_send()

    scale = math.log2(math.e) / math.sqrt(HEAD_WIDTH)

    def ids_of(slot):
        rows = kv[slot, 0:SEG_ROWS].astype(jnp.float32)
        return rows[0:1] * BASE + rows[1:2]

    def lower():
        return (lax.broadcasted_iota(jnp.int32, (tok, tok), 1)
                <= lax.broadcasted_iota(jnp.int32, (tok, tok), 0))

    def masks_a():
        cols = jnp.broadcast_to(ids_of(SPAN), (tok, tok))
        rows = jnp.transpose(cols)
        old = jnp.broadcast_to(ids_of(0), (tok, tok))
        tri_bias[...] = jnp.where(jnp.where(lower(), cols, old) == rows, 0.0, -BIG)
        pair_bias[...] = jnp.where(jnp.broadcast_to(ids_of(pair_slot), (tok, tok)) == rows, 0.0, -BIG)
        row_neg[...] = jnp.where(rows == rows[0:1, :], 0.0, -BIG)

    def dots(a, b):
        return lax.dot_general(a, b, (((1,), (1,)), ((), ())), preferred_element_type=jnp.float32)

    def queries(c, n):
        return jnp.concatenate(
            [q_buf[:, (c + g) * HEAD_WIDTH:(c + g + 1) * HEAD_WIDTH] for g in range(n)], 0)

    def part_a(h):
        tall = lambda x: jnp.concatenate([x] * group, 0)
        q = queries(h * group, group)
        tri2 = tall(lower())
        s_own = dots(q, kv[SPAN, key_rows(h, 0)])
        s_old = dots(q, kv[0, key_rows(h, 0)])
        s_pair = dots(q, kv[pair_slot, key_rows(h, 0)]) + tall(pair_bias[...])
        s_tri = jnp.where(tri2, s_own, s_old) + tall(tri_bias[...])
        top = jnp.max(jnp.maximum(s_tri, s_pair), axis=1, keepdims=True)
        p_tri = jnp.exp2((s_tri - top) * scale)
        p_pair = jnp.exp2((s_pair - top) * scale).astype(jnp.bfloat16)
        p_own = jnp.where(tri2, p_tri, 0.0).astype(jnp.bfloat16)
        p_old = jnp.where(tri2, 0.0, p_tri).astype(jnp.bfloat16)
        v_all = jnp.concatenate([kv[SPAN, key_rows(h, 1)], kv[0, key_rows(h, 1)],
                                 kv[pair_slot, key_rows(h, 1)]], 0)
        ones = jnp.ones((3 * tok, HEAD_WIDTH), jnp.bfloat16)
        out = jnp.dot(jnp.concatenate([p_own, p_old, p_pair], 1),
                      jnp.concatenate([v_all, ones], 1), preferred_element_type=jnp.float32)
        acc[h * group:(h + 1) * group] = out.reshape(group, tok, 2 * HEAD_WIDTH)
        top_a[h * group:(h + 1) * group] = jnp.broadcast_to(
            top, (group * tok, HEAD_WIDTH)).reshape(group, tok, HEAD_WIDTH)

    def part_b(h, starts, last, n=0, k=1):
        size = group // k
        c = h * group + n * size
        wide = 2 * len(starts) * tok
        tall = lambda x: jnp.concatenate([x] * size, 0)

        def gather(which):
            return jnp.concatenate(
                [kv[pl.ds(e, 2), key_rows(h, which)].reshape(2 * tok, HEAD_WIDTH) for e in starts], 0)

        s_mid = dots(queries(c, size), gather(0))
        neg = tall(row_neg[...])
        bias = [col_bias[e + r] for e in starts for r in range(2)]
        mids = [s_mid[:, r * tok:(r + 1) * tok] + b for r, b in enumerate(bias)]
        old = top_a[c:c + size].reshape(size * tok, HEAD_WIDTH)
        top = jnp.max(functools.reduce(jnp.maximum, mids) + neg, axis=1, keepdims=True)
        top = jnp.maximum(old, top)
        fade = jnp.exp2((old - top) * scale)
        lift = top - neg
        p_mid = [jnp.exp2((s - lift) * scale).astype(jnp.bfloat16) for s in mids]
        ones = jnp.ones((wide, HEAD_WIDTH), jnp.bfloat16)
        out = jnp.dot(jnp.concatenate(p_mid, 1), jnp.concatenate([gather(1), ones], 1),
                      preferred_element_type=jnp.float32)
        was = acc[c:c + size].reshape(size * tok, 2 * HEAD_WIDTH)
        value = out[:, :HEAD_WIDTH] + fade * was[:, :HEAD_WIDTH]
        total = out[:, HEAD_WIDTH:] + fade * was[:, HEAD_WIDTH:]
        if last:
            out = (value / total).astype(o_ref.dtype)
            for g in range(size):
                o_ref[:, (c + g) * HEAD_WIDTH:(c + g + 1) * HEAD_WIDTH] = out[g * tok:(g + 1) * tok]
        else:
            acc[c:c + size] = jnp.concatenate([value, total], 1).reshape(size, tok, 2 * HEAD_WIDTH)
            top_a[c:c + size] = top.reshape(size, tok, HEAD_WIDTH)

    pairs = [slot_at(o * 2, spot) for o in chips]

    def masks_b(which):
        head = jnp.broadcast_to(ids_of(SPAN)[:, 0:1], (1, tok))
        for m in which:
            for r in range(2):
                col_bias[pairs[m] + r] = jnp.where(ids_of(pairs[m] + r) == head, 0.0, -BIG)

    def take(p, m):
        if modes[p] == "G":
            plane(p, m)
        else:
            @pl.when(jnp.logical_or(low[m], has_prev))
            def _():
                wait_slot(p, here[m])
                if m == 1:
                    relay(p).start()
            share(p, m).start()

    def do_a(p):
        ready_pair(p)
        load_q(p).wait()
        if p == 0:
            masks_a()
        part_a(p)

    def do_near(p):
        for m in range(2):
            wait_slot(p, other[m])
        if p == 0:
            masks_b((0, 1))
        part_b(p, pairs[:2], False)

    def do_far(p):
        wait_slot(p, other[2])
        if p == 0:
            masks_b((2,))
        part_b(p, pairs[2:], True)

    open_next(0)
    open_own(0)
    open_next(2)
    open_own(2)
    open_next(3)
    open_own(3)
    open_next(1)
    open_own(1)
    open_prev(0)
    open_prev(2)
    do_a(0)
    open_prev(3)
    do_a(2)
    take(1,0)
    take(0,1)
    take(2,0)
    open_prev(1)
    take(1,1)
    take(0,0)
    take(2,1)
    do_a(3)
    do_a(1)
    take(3,1)
    take(3,0)
    do_near(0)
    take(1,2)
    take(0,2)
    do_near(2)
    settle(1,0)
    settle(1,1)
    take(2,2)
    do_near(3)
    take(3,2)
    do_far(0)
    settle(1,2)
    do_near(1)
    do_far(2)
    do_far(1)
    do_far(3)
    for p in range(4):
        finish(p)


def shards(count, cp_count, query_proj, key_proj, value_projection, segment_ids):
    tok = query_proj.shape[0]
    heads = key_proj.shape[1] // HEAD_WIDTH
    group = query_proj.shape[1] // key_proj.shape[1]
    inputs = (query_proj, key_proj, value_projection, segment_ids.reshape(1, tok))
    return pl.pallas_call(
        functools.partial(kernel, count, cp_count, heads, group),
        out_shape=pltpu.VMEM(query_proj.shape, query_proj.dtype),
        in_specs=[pl.BlockSpec(memory_space=pl.ANY)] * 4,
        out_specs=pl.BlockSpec(memory_space=pltpu.VMEM),
        scratch_shapes=[
            pltpu.VMEM((SPAN + 4, SEG_ROWS + 2 * heads * tok, HEAD_WIDTH), key_proj.dtype),
            pltpu.VMEM((1, tok), segment_ids.dtype),
            pltpu.VMEM(query_proj.shape, query_proj.dtype),
            pltpu.VMEM((heads * group, tok, 2 * HEAD_WIDTH), jnp.float32),
            pltpu.VMEM((heads * group, tok, HEAD_WIDTH), jnp.float32),
            pltpu.VMEM((tok, tok), jnp.float32),
            pltpu.VMEM((tok, tok), jnp.float32),
            pltpu.VMEM((tok, tok), jnp.float32),
            pltpu.VMEM((SPAN, 1, tok), jnp.float32),
            pltpu.SemaphoreType.DMA((4, SENDS)),
            pltpu.SemaphoreType.DMA((4, SPAN + 4)),
            pltpu.SemaphoreType.DMA((2 * heads + 1,)),
            pltpu.SemaphoreType.DMA((heads,)),
        ],
        compiler_params=pltpu.CompilerParams(
            collective_id=0, has_side_effects=True, vmem_limit_bytes=24 * 2**20),
        name="window_attention",
    )(*[pltpu.with_memory_space_constraint(x, pltpu.HBM) for x in inputs])


def solution(mesh):
    cp_count = mesh.shape["cp"]
    count = mesh.shape["grp"] * cp_count
    spec = P(("grp", "cp"), None)
    return jax.shard_map(
        functools.partial(shards, count, cp_count),
        mesh=mesh,
        in_specs=(spec, spec, spec, P(("grp", "cp"))),
        out_specs=spec,
        check_vma=False,
    )
```

```python
import functools
import math

import jax
import jax.numpy as jnp
from jax import lax
from jax.experimental import pallas as pl
from jax.experimental.pallas import tpu as pltpu
from jax.sharding import PartitionSpec as P

HEAD_WIDTH = 128
SPAN = 8
SEG_ROWS = 16
BASE = 16
BIG = 1e30
MESH = pl.DeviceIdType.MESH
NEXT, ACROSS, RELAY, PAIR, SHARE, UP = 0, 1, 4, 5, 6, 9
SENDS = 12


def kernel(
    count, cp_count, heads, group,
    q_hbm, k_hbm, v_hbm, s_hbm, o_ref,
    kv, seg, q_buf, acc, top_a, tri_bias, pair_bias, row_neg, col_bias,
    send_sem, recv_sem, in_sem, q_sem,
):
    tok = q_buf.shape[0]
    flat = lax.axis_index("grp") * cp_count + lax.axis_index("cp")
    spot = lax.rem(flat, SPAN)
    base = flat - spot
    chip, core = spot // 2, lax.rem(spot, 2)
    mate = chip * 2 + 1 - core
    has_prev = flat >= SPAN
    has_next = flat + SPAN < count
    chips = [jnp.bitwise_xor(chip, m) for m in (1, 2, 3)]
    spots = [o * 2 + core for o in chips]
    modes = 'RGRR'
    parts = len(modes)
    cuts = [0, 1, 2, 3, 4]

    def dev(f):
        return (f // cp_count, lax.rem(f, cp_count))

    def slot_at(owner, place):
        return lax.rem(owner - place + SPAN, SPAN)

    mate_dev = dev(base + mate)
    next_dev, prev_dev = dev(flat + SPAN), dev(flat - SPAN)
    side_dev = [dev(base + t) for t in spots]
    low = [o < chip for o in chips]
    high = [o > chip for o in chips]
    there = [slot_at(spot, t) for t in spots]
    shared = [slot_at(t, mate) for t in spots]
    other = [slot_at(o * 2 + 1 - core, spot) for o in chips]
    here = [slot_at(s, spot) for s in spots]
    pair_slot = slot_at(mate, spot)
    pair_dst = slot_at(spot, mate)
    pair_src = jnp.where(core == 0, SPAN, 0)
    side_src = [jnp.where(x, 0, SPAN) for x in low]
    arrivals = [jnp.where(low[m], here[m], SPAN + 1 + m) for m in range(3)]
    early_dst = [jnp.where(low[m], SPAN + 1 + m, there[m]) for m in range(3)]
    x_relay = jnp.where(chips[0] < chips[1], slot_at(spots[0], spots[1]), SPAN + 3)
    y_relay = slot_at(spots[1], spots[0])

    def span_of(p):
        begin = SEG_ROWS + 2 * tok * cuts[p] if p else 0
        return pl.ds(begin, SEG_ROWS + 2 * tok * cuts[p + 1] - begin)

    def view(p, slot):
        return kv.at[slot, span_of(p)]

    def remote(h, src, dst, k, target):
        return pltpu.make_async_remote_copy(
            src_ref=view(h, src), dst_ref=view(h, dst),
            send_sem=send_sem.at[h, k], recv_sem=recv_sem.at[h, dst],
            device_id=target, device_id_type=MESH,
        )

    def wait_slot(h, slot):
        remote(h, SPAN, slot, 0, mate_dev).wait_recv()

    def key_rows(h, which):
        return pl.ds(SEG_ROWS + (2 * h + which) * tok, tok)

    def load_in(h, which):
        ref = (k_hbm, v_hbm)[which]
        return pltpu.make_async_copy(
            ref.at[:, h * HEAD_WIDTH:(h + 1) * HEAD_WIDTH], kv.at[SPAN, key_rows(h, which)],
            in_sem.at[2 * h + which])

    width = group * HEAD_WIDTH

    def load_q(h):
        return pltpu.make_async_copy(
            q_hbm.at[:, h * width:(h + 1) * width], q_buf.at[:, h * width:(h + 1) * width],
            q_sem.at[h])

    seg_in = pltpu.make_async_copy(s_hbm, seg, in_sem.at[2 * heads])
    seg_in.start()
    for h in range(heads):
        for which in range(2):
            load_in(h, which).start()

    barrier = pltpu.get_barrier_semaphore()

    def hello(target):
        pl.semaphore_signal(barrier, inc=1, device_id=target, device_id_type=MESH)

    for t in [mate_dev] + side_dev:
        hello(t)

    @pl.when(has_prev)
    def _():
        hello(prev_dev)

    @pl.when(has_next)
    def _():
        hello(next_dev)

    for h in range(heads):
        load_q(h).start()

    @pl.when(jnp.logical_not(has_prev))
    def _():
        kv[0] = jnp.full(kv.shape[1:], -1, kv.dtype)
        for m in range(3):
            @pl.when(high[m])
            def _():
                kv[here[m]] = jnp.full(kv.shape[1:], -1, kv.dtype)

    seg_in.wait()
    ids = seg[...]
    line = lax.broadcasted_iota(jnp.int32, (SEG_ROWS, tok), 0)
    kv[SPAN, 0:SEG_ROWS] = jnp.where(
        line == 0, ids // BASE, jnp.where(line == 1, ids % BASE, 0)
    ).astype(jnp.float32).astype(kv.dtype)

    pl.semaphore_wait(
        barrier, 4 + has_prev.astype(jnp.int32) + has_next.astype(jnp.int32))

    def to_next(h):
        return remote(h, SPAN, 0, NEXT, next_dev)

    def direct(h, m):
        if modes[h] == "G":
            return remote(h, SPAN, early_dst[m], ACROSS + m, side_dev[m])
        return remote(h, side_src[m], there[m], ACROSS + m, side_dev[m])

    def relay(h):
        if modes[h] == "G":
            return remote(h, arrivals[0], x_relay, RELAY, side_dev[1])
        return remote(h, here[1], y_relay, RELAY, side_dev[0])

    def to_mate(h):
        return remote(h, pair_src, pair_dst, PAIR, mate_dev)

    def share(h, m):
        return remote(h, here[m], shared[m], SHARE + m, mate_dev)

    def up(h, m):
        return remote(h, SPAN + 1 + m, here[m], UP + m, next_dev)

    def loaded(p):
        for h in range(cuts[p], cuts[p + 1]):
            load_in(h, 0).wait()
            load_in(h, 1).wait()

    def open_next(h):
        loaded(h)

        @pl.when(has_next)
        def _():
            to_next(h).start()

    def open_own(h):
        for m in range(2):
            if modes[h] == "G":
                direct(h, m).start()
            else:
                @pl.when(high[m])
                def _():
                    direct(h, m).start()

        @pl.when(core == 0)
        def _():
            to_mate(h).start()

    def open_prev(h):
        @pl.when(has_prev)
        def _():
            wait_slot(h, 0)
            if modes[h] != "G":
                for m in range(2):
                    @pl.when(low[m])
                    def _():
                        direct(h, m).start()

        @pl.when(core == 1)
        def _():
            to_mate(h).start()

    def plane(h, m):
        wait_slot(h, arrivals[m])
        if m == 0:
            relay(h).start()

        @pl.when(jnp.logical_and(high[m], has_next))
        def _():
            up(h, m).start()

        @pl.when(low[m])
        def _():
            share(h, m).start()

    def settle(h, m):
        @pl.when(high[m])
        def _():
            @pl.when(has_prev)
            def _():
                wait_slot(h, here[m])
            share(h, m).start()

    def ready_pair(h):
        wait_slot(h, pair_slot)

    def finish(h):
        @pl.when(has_next)
        def _():
            to_next(h).wait_send()
        if modes[h] == "G":
            for m in range(2):
                direct(h, m).wait_send()
            relay(h).wait_send()
        else:
            for m in range(2):
                @pl.when(jnp.logical_or(high[m], has_prev))
                def _():
                    direct(h, m).wait_send()

            @pl.when(jnp.logical_or(low[1], has_prev))
            def _():
                relay(h).wait_send()
        to_mate(h).wait_send()
        for m in range(3):
            share(h, m).wait_send()
            if modes[h] == "G":
                @pl.when(jnp.logical_and(high[m], has_next))
                def _():
                    up(h, m).wait_send()

    scale = math.log2(math.e) / math.sqrt(HEAD_WIDTH)

    def ids_of(slot):
        rows = kv[slot, 0:SEG_ROWS].astype(jnp.float32)
        return rows[0:1] * BASE + rows[1:2]

    def lower():
        return (lax.broadcasted_iota(jnp.int32, (tok, tok), 1)
                <= lax.broadcasted_iota(jnp.int32, (tok, tok), 0))

    def masks_a():
        cols = jnp.broadcast_to(ids_of(SPAN), (tok, tok))
        rows = jnp.transpose(cols)
        old = jnp.broadcast_to(ids_of(0), (tok, tok))
        tri_bias[...] = jnp.where(jnp.where(lower(), cols, old) == rows, 0.0, -BIG)
        pair_bias[...] = jnp.where(jnp.broadcast_to(ids_of(pair_slot), (tok, tok)) == rows, 0.0, -BIG)
        row_neg[...] = jnp.where(rows == rows[0:1, :], 0.0, -BIG)

    def dots(a, b):
        return lax.dot_general(a, b, (((1,), (1,)), ((), ())), preferred_element_type=jnp.float32)

    def queries(c, n):
        return jnp.concatenate(
            [q_buf[:, (c + g) * HEAD_WIDTH:(c + g + 1) * HEAD_WIDTH] for g in range(n)], 0)

    def part_a(h):
        tall = lambda x: jnp.concatenate([x] * group, 0)
        q = queries(h * group, group)
        tri2 = tall(lower())
        s_own = dots(q, kv[SPAN, key_rows(h, 0)])
        s_old = dots(q, kv[0, key_rows(h, 0)])
        s_pair = dots(q, kv[pair_slot, key_rows(h, 0)]) + tall(pair_bias[...])
        s_tri = jnp.where(tri2, s_own, s_old) + tall(tri_bias[...])
        top = jnp.max(jnp.maximum(s_tri, s_pair), axis=1, keepdims=True)
        p_tri = jnp.exp2((s_tri - top) * scale)
        p_pair = jnp.exp2((s_pair - top) * scale).astype(jnp.bfloat16)
        p_own = jnp.where(tri2, p_tri, 0.0).astype(jnp.bfloat16)
        p_old = jnp.where(tri2, 0.0, p_tri).astype(jnp.bfloat16)
        v_all = jnp.concatenate([kv[SPAN, key_rows(h, 1)], kv[0, key_rows(h, 1)],
                                 kv[pair_slot, key_rows(h, 1)]], 0)
        ones = jnp.ones((3 * tok, HEAD_WIDTH), jnp.bfloat16)
        out = jnp.dot(jnp.concatenate([p_own, p_old, p_pair], 1),
                      jnp.concatenate([v_all, ones], 1), preferred_element_type=jnp.float32)
        acc[h * group:(h + 1) * group] = out.reshape(group, tok, 2 * HEAD_WIDTH)
        top_a[h * group:(h + 1) * group] = jnp.broadcast_to(
            top, (group * tok, HEAD_WIDTH)).reshape(group, tok, HEAD_WIDTH)

    def part_b(h, starts, last, n=0, k=1):
        size = group // k
        c = h * group + n * size
        wide = 2 * len(starts) * tok
        tall = lambda x: jnp.concatenate([x] * size, 0)

        def gather(which):
            return jnp.concatenate(
                [kv[pl.ds(e, 2), key_rows(h, which)].reshape(2 * tok, HEAD_WIDTH) for e in starts], 0)

        s_mid = dots(queries(c, size), gather(0))
        neg = tall(row_neg[...])
        bias = [col_bias[e + r] for e in starts for r in range(2)]
        mids = [s_mid[:, r * tok:(r + 1) * tok] + b for r, b in enumerate(bias)]
        old = top_a[c:c + size].reshape(size * tok, HEAD_WIDTH)
        top = jnp.max(functools.reduce(jnp.maximum, mids) + neg, axis=1, keepdims=True)
        top = jnp.maximum(old, top)
        fade = jnp.exp2((old - top) * scale)
        lift = top - neg
        p_mid = [jnp.exp2((s - lift) * scale).astype(jnp.bfloat16) for s in mids]
        ones = jnp.ones((wide, HEAD_WIDTH), jnp.bfloat16)
        out = jnp.dot(jnp.concatenate(p_mid, 1), jnp.concatenate([gather(1), ones], 1),
                      preferred_element_type=jnp.float32)
        was = acc[c:c + size].reshape(size * tok, 2 * HEAD_WIDTH)
        value = out[:, :HEAD_WIDTH] + fade * was[:, :HEAD_WIDTH]
        total = out[:, HEAD_WIDTH:] + fade * was[:, HEAD_WIDTH:]
        if last:
            out = (value / total).astype(o_ref.dtype)
            for g in range(size):
                o_ref[:, (c + g) * HEAD_WIDTH:(c + g + 1) * HEAD_WIDTH] = out[g * tok:(g + 1) * tok]
        else:
            acc[c:c + size] = jnp.concatenate([value, total], 1).reshape(size, tok, 2 * HEAD_WIDTH)
            top_a[c:c + size] = top.reshape(size, tok, HEAD_WIDTH)

    pairs = [slot_at(o * 2, spot) for o in chips]

    def masks_b(which):
        head = jnp.broadcast_to(ids_of(SPAN)[:, 0:1], (1, tok))
        for m in which:
            for r in range(2):
                col_bias[pairs[m] + r] = jnp.where(ids_of(pairs[m] + r) == head, 0.0, -BIG)

    def take(p, m):
        if modes[p] == "G":
            plane(p, m)
        else:
            @pl.when(jnp.logical_or(low[m], has_prev))
            def _():
                wait_slot(p, here[m])
                if m == 1:
                    relay(p).start()
            share(p, m).start()

    def do_a(p):
        ready_pair(p)
        load_q(p).wait()
        if p == 0:
            masks_a()
        part_a(p)

    def do_near(p):
        for m in range(2):
            wait_slot(p, other[m])
        if p == 0:
            masks_b((0, 1))
        part_b(p, pairs[:2], False)

    def do_far(p):
        wait_slot(p, other[2])
        if p == 0:
            masks_b((2,))
        part_b(p, pairs[2:], True)

    open_next(0)
    open_own(0)
    open_next(2)
    open_own(2)
    open_next(3)
    open_own(3)
    open_next(1)
    open_own(1)
    open_prev(0)
    open_prev(2)
    do_a(0)
    open_prev(3)
    do_a(2)
    take(1,0)
    take(0,1)
    take(2,0)
    open_prev(1)
    take(1,1)
    take(0,0)
    do_a(3)
    take(2,1)
    do_a(1)
    take(3,1)
    take(3,0)
    do_near(0)
    take(1,2)
    take(0,2)
    do_near(2)
    settle(1,0)
    settle(1,1)
    take(2,2)
    do_near(3)
    take(3,2)
    do_far(0)
    settle(1,2)
    do_near(1)
    do_far(2)
    do_far(1)
    do_far(3)
    for p in range(4):
        finish(p)


def shards(count, cp_count, query_proj, key_proj, value_projection, segment_ids):
    tok = query_proj.shape[0]
    heads = key_proj.shape[1] // HEAD_WIDTH
    group = query_proj.shape[1] // key_proj.shape[1]
    inputs = (query_proj, key_proj, value_projection, segment_ids.reshape(1, tok))
    return pl.pallas_call(
        functools.partial(kernel, count, cp_count, heads, group),
        out_shape=pltpu.VMEM(query_proj.shape, query_proj.dtype),
        in_specs=[pl.BlockSpec(memory_space=pl.ANY)] * 4,
        out_specs=pl.BlockSpec(memory_space=pltpu.VMEM),
        scratch_shapes=[
            pltpu.VMEM((SPAN + 4, SEG_ROWS + 2 * heads * tok, HEAD_WIDTH), key_proj.dtype),
            pltpu.VMEM((1, tok), segment_ids.dtype),
            pltpu.VMEM(query_proj.shape, query_proj.dtype),
            pltpu.VMEM((heads * group, tok, 2 * HEAD_WIDTH), jnp.float32),
            pltpu.VMEM((heads * group, tok, HEAD_WIDTH), jnp.float32),
            pltpu.VMEM((tok, tok), jnp.float32),
            pltpu.VMEM((tok, tok), jnp.float32),
            pltpu.VMEM((tok, tok), jnp.float32),
            pltpu.VMEM((SPAN, 1, tok), jnp.float32),
            pltpu.SemaphoreType.DMA((4, SENDS)),
            pltpu.SemaphoreType.DMA((4, SPAN + 4)),
            pltpu.SemaphoreType.DMA((2 * heads + 1,)),
            pltpu.SemaphoreType.DMA((heads,)),
        ],
        compiler_params=pltpu.CompilerParams(
            collective_id=0, has_side_effects=True, vmem_limit_bytes=24 * 2**20),
        name="window_attention",
    )(*[pltpu.with_memory_space_constraint(x, pltpu.HBM) for x in inputs])


def solution(mesh):
    cp_count = mesh.shape["cp"]
    count = mesh.shape["grp"] * cp_count
    spec = P(("grp", "cp"), None)
    return jax.shard_map(
        functools.partial(shards, count, cp_count),
        mesh=mesh,
        in_specs=(spec, spec, spec, P(("grp", "cp"))),
        out_specs=spec,
        check_vma=False,
    )
```
